32 devices in a mesh: dp: 8 (over y, x, core), fsdp: 4 (over z).
Axes of the slice: x: 2, y: 2, z: 4, core: 2. Of those that a mesh axis runs over, the one named last changes fastest.
Arguments:
- tokens: bfloat16 [16384, 1152], P(('dp', 'fsdp')), may hold values from -6 to 6
- lengths: int32 [8, 3], P('dp'), may hold values from 1 to 1024, 2048 in all within a row
- w_q: bfloat16 [1152, 1024], P('fsdp'), may hold values from -0.1875 to 0.1875
- w_k: bfloat16 [1152, 256], P('fsdp'), may hold values from -0.1875 to 0.1875
- w_v: bfloat16 [1152, 256], P('fsdp'), may hold values from -0.1875 to 0.1875
- w_o: bfloat16 [1024, 1152], P('fsdp'), may hold values from -0.1875 to 0.1875
- w_gate: bfloat16 [1152, 6912], P(None, 'fsdp'), may hold values from -0.1875 to 0.1875
- w_up: bfloat16 [1152, 6912], P(None, 'fsdp'), may hold values from -0.1875 to 0.1875
- w_down: bfloat16 [6912, 1152], P('fsdp'), may hold values from -0.078125 to 0.078125
- g_attn: float32 [1152], replicated, may hold values from 0.1 to 1.9
- g_q: float32 [256], replicated, may hold values from 0.1 to 1.9
- g_k: float32 [256], replicated, may hold values from 0.1 to 1.9
- g_post_attn: float32 [1152], replicated, may hold values from 0.1 to 1.9
- g_ffn: float32 [1152], replicated, may hold values from 0.1 to 1.9
- g_post_ffn: float32 [1152], replicated, may hold values from 0.1 to 1.9
- cotangent: bfloat16 [16384, 1152], P(('dp', 'fsdp')), may hold values from -6 to 6
Outputs:
- output: bfloat16 [16384, 1152], P(('dp', 'fsdp'))
- grad_tokens: bfloat16 [16384, 1152], P(('dp', 'fsdp'))
- grad_w_q: float32 [1152, 1024], P('fsdp', 'dp')
- grad_w_k: float32 [1152, 256], P('fsdp', 'dp')
- grad_w_v: float32 [1152, 256], P('fsdp', 'dp')
- grad_w_o: float32 [1024, 1152], P('fsdp', 'dp')
- grad_w_gate: float32 [1152, 6912], P('dp', 'fsdp')
- grad_w_up: float32 [1152, 6912], P('dp', 'fsdp')
- grad_w_down: float32 [6912, 1152], P('fsdp', 'dp')
- grad_g_attn: float32 [1152], replicated
- grad_g_q: float32 [256], replicated
- grad_g_k: float32 [256], replicated
- grad_g_post_attn: float32 [1152], replicated
- grad_g_ffn: float32 [1152], replicated
- grad_g_post_ffn: float32 [1152], replicated
The draws below stay inside these ranges and needn't reach their ends.
Inputs may be any that keep to these rules, and one draw needn't show every extreme that they name: Each group's lengths sum to 2048; in each group the longest is exactly 1024.
All inputs are finite; a program needn't handle non-finite values.
Results may differ from the reference program's by a relative error of at most 0.019.
Values may be sent and summed in bfloat16 or wider, within the bound.
No kernel may reach another device: no remote copies, remote signals or barrier semaphores. Data moves between devices by JAX's collectives and lax.ppermute only.
A program may use at most 256 MiB of HBM per device.

```python
import math
import jax
import jax.numpy as jnp
import numpy as np
from jax import lax

D = 1152
HEADS = 4
HEAD = 256
FF = 6912
WINDOW = 512
SEQS = 3
GROUP_TOK = 2048
MAX_LEN = 1024
TOKENS = 16384
N_DP = 8


def shard_levels(key, dims, pieces, smallest, largest):
    level = 1.0
    for dim, blocks in pieces:
        draws = jax.random.uniform(jax.random.fold_in(jax.random.fold_in(key, 6), dim), (blocks,), jnp.float32, smallest / len(pieces), largest / len(pieces))
        level = level * jnp.repeat(jnp.exp(draws), dims[dim] // blocks).reshape((-1,) + (1,) * (len(dims) - 1 - dim))
    return level


def length_profile(number_of, total, reach, skew):
    portions = [(1 << 20) // math.isqrt(grade ** skew) + 1 for grade in range(2, number_of + 1)]
    surplus, holding = total - reach - (number_of - 1), [1] * (number_of - 1)
    while surplus > 0:
        candidates = [i for i in range(number_of - 1) if holding[i] < reach]
        whole, remaining = sum([portions[i] for i in candidates]), surplus
        for i in candidates:
            extra = min(reach - holding[i], max(1, remaining * portions[i] // whole), surplus)
            holding[i] = holding[i] + extra
            surplus = surplus - extra
    return np.array([reach] + holding)


def ragged_sizes(rng, number_of, total, bound, skew):
    if number_of == 2:
        one = jax.random.randint(rng, (), max(1, total - bound), min(bound, total - 1) + 1)
        return jnp.stack([one, total - one])
    sizes = jnp.asarray(length_profile(number_of, total, bound, skew), jnp.int32)
    pairs = (number_of - 1) // 2
    source_of, sink = sizes[1:1 + 2 * pairs:2], sizes[2:2 + 2 * pairs:2]
    slack = jnp.minimum(source_of - 1, bound - sink)
    moved = jax.random.randint(jax.random.fold_in(rng, 1), (pairs,), 0, 1 << 20) % (slack + 1)
    sizes = sizes.at[1:1 + 2 * pairs:2].set(source_of - moved).at[2:2 + 2 * pairs:2].set(sink + moved)
    return sizes[jax.random.permutation(jax.random.fold_in(rng, 2), number_of)]


def bell_draw(key, extent, spread, reach, pieces=(), kind=jnp.bfloat16):
    factor_of = shard_levels(key, extent, pieces, -0.22, 0.18) if pieces else 1.0
    array = jax.random.normal(key, extent, jnp.float32) * spread * factor_of
    return jnp.minimum(jnp.maximum(array, -reach), reach).astype(kind)


def setup_inputs(seed: int = 0) -> dict:
    key_list = jax.random.split(jax.random.key(seed), 17)
    tokens = bell_draw(key_list[0], (TOKENS, D), 1.0, 6.0, ((0, 32),))
    lengths = jax.vmap(lambda own: ragged_sizes(own, SEQS, GROUP_TOK, MAX_LEN, 2))(jax.random.split(key_list[1], N_DP)).reshape((N_DP, SEQS)).astype(jnp.int32)
    w_q = bell_draw(key_list[2], (D, HEADS * HEAD), D ** -0.5, 0.1875, ((0, 4),))
    w_k = bell_draw(key_list[3], (D, HEAD), D ** -0.5, 0.1875, ((0, 4),))
    w_v = bell_draw(key_list[4], (D, HEAD), D ** -0.5, 0.1875, ((0, 4),))
    w_o = bell_draw(key_list[5], (HEADS * HEAD, D), (HEADS * HEAD) ** -0.5, 0.1875, ((0, 4),))
    w_gate = bell_draw(key_list[6], (D, FF), D ** -0.5, 0.1875, ((1, 4),))
    w_up = bell_draw(key_list[7], (D, FF), D ** -0.5, 0.1875, ((1, 4),))
    w_down = bell_draw(key_list[8], (FF, D), FF ** -0.5, 0.078125, ((0, 4),))
    g_attn = jnp.clip(1.0 + 0.18 * jax.random.normal(key_list[9], (D,), jnp.float32), 0.1, 1.9)
    g_q = jnp.clip(1.0 + 0.18 * jax.random.normal(key_list[10], (HEAD,), jnp.float32), 0.1, 1.9)
    g_k = jnp.clip(1.0 + 0.18 * jax.random.normal(key_list[11], (HEAD,), jnp.float32), 0.1, 1.9)
    g_post_attn = jnp.clip(1.0 + 0.18 * jax.random.normal(key_list[12], (D,), jnp.float32), 0.1, 1.9)
    g_ffn = jnp.clip(1.0 + 0.18 * jax.random.normal(key_list[13], (D,), jnp.float32), 0.1, 1.9)
    g_post_ffn = jnp.clip(1.0 + 0.18 * jax.random.normal(key_list[14], (D,), jnp.float32), 0.1, 1.9)
    cotangent = bell_draw(key_list[15], (TOKENS, D), 1.0, 6.0, ((0, 32),))
    return {"tokens": tokens, "lengths": lengths, "w_q": w_q, "w_k": w_k, "w_v": w_v, "w_o": w_o, "w_gate": w_gate, "w_up": w_up, "w_down": w_down, "g_attn": g_attn, "g_q": g_q, "g_k": g_k, "g_post_attn": g_post_attn, "g_ffn": g_ffn, "g_post_ffn": g_post_ffn, "cotangent": cotangent}


epsilon = 1e-06
rope_base = 10000.0
masked_score = -1e+30

@jax.custom_vjp
def low(v):
    return lax.optimization_barrier(v.astype(jnp.bfloat16)).astype(jnp.float32)

@jax.custom_vjp
def low_back(v):
    return v

def low_keep(v):
    return (low(v), None)

def low_pass(kept, grad):
    return (grad,)

def back_keep(v):
    return (v, None)

def back_low(kept, grad):
    return (low(grad),)
low.defvjp(low_keep, low_pass)
low_back.defvjp(back_keep, back_low)

def product(left_rows, right_rows):
    return jnp.dot(left_rows, right_rows, precision=lax.Precision.HIGHEST, preferred_element_type=jnp.float32)

def norm_rows(value, gain_vec):
    return value * lax.rsqrt(lax.optimization_barrier(jnp.mean(value * value, axis=-1, keepdims=True)) + epsilon) * gain_vec

def rotate(value, cos_table, sin_table):
    half_size = value.shape[-1] // 2
    turned = jnp.concatenate([-value[..., half_size:], value[..., :half_size]], axis=-1)
    return value * cos_table + turned * sin_table

def rope_tables(position, head_size):
    inverse_freq = rope_base ** (-jnp.arange(0, head_size, 2, dtype=jnp.float32) / head_size)
    angles = position.astype(jnp.float32)[:, None] * inverse_freq[None, :]
    angles = jnp.concatenate([angles, angles], axis=-1)
    return (jnp.cos(angles), jnp.sin(angles))

def seq_layout(lengths_row, index):
    seq_ends = jnp.cumsum(lengths_row)
    starts = seq_ends - lengths_row
    segment = lax.optimization_barrier(jnp.sum((index[:, None] >= seq_ends[None, :]).astype(jnp.int32), axis=1))
    chosen = segment[:, None] == jnp.arange(lengths_row.shape[0], dtype=jnp.int32)[None, :]
    seq_start = lax.optimization_barrier(jnp.sum(jnp.where(chosen, starts[None, :], 0), axis=1))
    return (segment, index - seq_start)

def visible(seg_query, seg_key, pos_query, pos_key):
    distance = pos_query[:, None] - pos_key[None, :]
    return (seg_query[:, None] == seg_key[None, :]) & (distance >= 0) & (distance < WINDOW)

def pair_blocks(table):
    block_count = (table.shape[0] - WINDOW) // WINDOW
    earlier = table[:-WINDOW].reshape((block_count, WINDOW) + table.shape[1:])
    current = table[WINDOW:].reshape((block_count, WINDOW) + table.shape[1:])
    return jnp.concatenate([earlier, current], axis=1)

def attend_block(block_items):
    queries, key_rows, value_rows, seg_query, seg_key, pos_query, pos_key = block_items
    scores = jnp.einsum('qhd,kd->hqk', queries, key_rows, precision=lax.Precision.HIGHEST) * HEAD ** (-0.5)
    scores = low_back(scores)
    allowed = visible(seg_query, seg_key, pos_query, pos_key)
    scores = jnp.where(allowed[None], scores, masked_score)
    row_max = lax.optimization_barrier(jnp.max(scores, axis=-1, keepdims=True))
    weights_exp = jnp.exp(scores - row_max)
    chance = low(weights_exp / lax.optimization_barrier(jnp.sum(weights_exp, axis=-1, keepdims=True)))
    return jnp.einsum('hqk,kd->qhd', chance, value_rows, precision=lax.Precision.HIGHEST)

def attend(queries, key_rows, value_rows, segment, position):
    total_rows = segment.shape[0]
    block_count = total_rows // WINDOW

    def extend(table, filler):
        padding = jnp.full((WINDOW,) + table.shape[1:], filler, table.dtype)
        return pair_blocks(jnp.concatenate([padding, table]))
    block_items = (queries.reshape(block_count, WINDOW, HEADS, HEAD), extend(key_rows, 0.0), extend(value_rows, 0.0), segment.reshape(block_count, WINDOW), extend(segment, -1), position.reshape(block_count, WINDOW), extend(position, 0))
    mixture = lax.map(jax.checkpoint(attend_block), block_items)
    return mixture.reshape(total_rows, HEADS * HEAD)

def layer(inputs, params, segment, position):
    w_q, w_k, w_v, w_o, w_gate, w_up, w_down, g_attn, g_q, g_k, g_post_attn, g_ffn, g_post_ffn = params
    total_rows = inputs.shape[0]
    cos_table, sin_table = rope_tables(position, HEAD)
    normed_in = low(norm_rows(inputs, g_attn))
    q_raw = low_back(product(normed_in, w_q)).reshape(total_rows, HEADS, HEAD)
    k_raw = low_back(product(normed_in, w_k))
    value_rows = low(low_back(product(normed_in, w_v)))
    queries = low(rotate(norm_rows(q_raw, g_q), cos_table[:, None, :], sin_table[:, None, :]))
    key_rows = low(rotate(norm_rows(k_raw, g_k), cos_table, sin_table))
    mixture = low(low_back(attend(queries, key_rows, value_rows, segment, position)))
    attn_out = low_back(product(mixture, w_o))
    residual = inputs + norm_rows(attn_out, g_post_attn)
    normed_mid = low(norm_rows(residual, g_ffn))
    gate_pre = low_back(product(normed_mid, w_gate))
    up_pre = low_back(product(normed_mid, w_up))
    hidden = low(jax.nn.gelu(gate_pre, approximate=True) * up_pre)
    branch = low_back(product(hidden, w_down))
    return residual + norm_rows(branch, g_post_ffn)

def reference(tokens, lengths, w_q, w_k, w_v, w_o, w_gate, w_up, w_down, g_attn, g_q, g_k, g_post_attn, g_ffn, g_post_ffn, cotangent):
    params = (w_q.astype(jnp.float32), w_k.astype(jnp.float32), w_v.astype(jnp.float32), w_o.astype(jnp.float32), w_gate.astype(jnp.float32), w_up.astype(jnp.float32), w_down.astype(jnp.float32), g_attn, g_q, g_k, g_post_attn, g_ffn, g_post_ffn)
    group_inputs = tokens.astype(jnp.float32).reshape(N_DP, GROUP_TOK, D)
    group_grads = cotangent.astype(jnp.float32).reshape(N_DP, GROUP_TOK, D)

    def step(running, record):
        inputs, grad_rows, lengths_row = record
        segment, position = seq_layout(lengths_row, jnp.arange(GROUP_TOK, dtype=jnp.int32))

        def forward(inner_inputs, *inner_params):
            return layer(inner_inputs, inner_params, segment, position)
        output, pull = jax.vjp(forward, inputs, *params)
        gradients = pull(grad_rows)
        running = tuple((total_grad + new_grad for total_grad, new_grad in zip(running, gradients[1:])))
        return (running, (output.astype(jnp.bfloat16), gradients[0].astype(jnp.bfloat16)))
    start_sums = tuple((jnp.zeros_like(param) for param in params))
    sums, (outputs, input_grads) = lax.scan(step, start_sums, (group_inputs, group_grads, lengths))
    return (outputs.reshape(TOKENS, D), input_grads.reshape(TOKENS, D), sums[0], sums[1], sums[2], sums[3], sums[4], sums[5], sums[6], sums[7], sums[8], sums[9], sums[10], sums[11], sums[12])
```

```python
import functools

import jax
import jax.numpy as jnp
import numpy as np
from jax import lax
from jax.experimental import pallas as pl
from jax.experimental.pallas import tpu as pltpu
from jax.sharding import PartitionSpec as P

WINDOW = 512
epsilon = 1e-06
rope_base = 10000.0
masked_score = -1e30
bf16, f32 = jnp.bfloat16, jnp.float32


def swap(x, axis, mask):
    return lax.ppermute(x, axis, [(i, i ^ mask) for i in range(lax.axis_size(axis))])


def passed_along(x, axis, by):
    length = lax.axis_size(axis)
    pairs = [(i, i + by) for i in range(length) if 0 <= i + by < length]
    return lax.ppermute(x, axis, pairs)


def plane_bits():
    bits, bit = [], 2
    while bit < lax.axis_size("dp"):
        bits.append(bit)
        bit *= 2
    return bits


def relative_order():
    digits = [1] + plane_bits()
    masks = []
    for place in range(lax.axis_size("dp")):
        mask = 0
        for rank, bit in enumerate(digits):
            if place >> (len(digits) - 1 - rank) & 1:
                mask |= bit
        masks.append(mask)
    return np.array(masks, np.int32)


def plane_orders():
    bits = plane_bits()
    return bits, bits[::-1]


def gather_plane(piece, order):
    bits = plane_bits()
    table = piece.reshape((1,) * len(bits) + piece.shape)
    for bit in order:
        table = jnp.concatenate([table, swap(table, "dp", bit)], axis=bits.index(bit))
    return table


def gather_core(table):
    return jnp.stack([table, swap(table, "dp", 1)])


def reduce_plane(keep, send, order, bits):
    left = list(bits)
    for place, bit in enumerate(order):
        left.remove(bit)
        total = keep.astype(f32) + swap(send.astype(bf16), "dp", bit).astype(f32)
        if place + 1 < len(order):
            following = left.index(order[place + 1])
            keep = lax.index_in_dim(total, 0, following, False)
            send = lax.index_in_dim(total, 1, following, False)
    return total


def reduce_halves(table, axis):
    bits = plane_bits()
    table = table.reshape((2,) * (1 + len(bits)) + table.shape[-2:])
    total = table[0].astype(f32) + swap(table[1].astype(bf16), "dp", 1).astype(f32)
    middle = (table.shape[-1] // 2 + 127) // 128 * 128
    parts = []
    for order, part in zip(plane_orders(), (total[..., :middle], total[..., middle:])):
        first = bits.index(order[0])
        keep = lax.index_in_dim(part, 0, first, False)
        send = lax.index_in_dim(part, 1, first, False)
        parts.append(reduce_plane(keep, send, order, bits))
    return jnp.concatenate(parts, axis=-1)


def scatter_shards(total, shards, me):
    rows, width = total.shape
    cols = width // shards

    def block(of):
        return lax.dynamic_slice(total, (0, of * cols), (rows, cols))

    out = block(me)
    for mask in range(1, shards):
        out = out + swap(block(me ^ mask).astype(bf16), "fsdp", mask).astype(f32)
    return out


def in_order(pieces, me):
    table = jnp.stack(pieces)
    shards = len(pieces)
    bit = 1
    while bit < shards:
        view = table.reshape((shards // (2 * bit), 2, bit) + table.shape[1:])
        table = jnp.where((me & bit) == 0, view, view[:, ::-1]).reshape(table.shape)
        bit *= 2
    return table


def shards_of(piece, me):
    shards = lax.axis_size("fsdp")
    return in_order([piece] + [swap(piece, "fsdp", mask) for mask in range(1, shards)], me)


def widths(total, chunk):
    count = -(-total // chunk)
    return count, total - (count - 1) * chunk


def reorder_rows(matrix, order, blocks):
    rows, cols = matrix.shape
    size = rows // blocks
    if size % 16:
        return jnp.take(matrix.reshape(blocks, size, cols), order, axis=0).reshape(rows, cols)

    def kernel(order_ref, in_ref, out_ref):
        out_ref[...] = in_ref[...]

    return pl.pallas_call(
        kernel,
        out_shape=jax.ShapeDtypeStruct(matrix.shape, matrix.dtype),
        grid_spec=pltpu.PrefetchScalarGridSpec(
            num_scalar_prefetch=1,
            grid=(blocks,),
            in_specs=[pl.BlockSpec((size, cols), lambda i, order: (order[i], 0))],
            out_specs=pl.BlockSpec((size, cols), lambda i, order: (i, 0)),
        ),
        cost_estimate=pl.CostEstimate(flops=0, bytes_accessed=4 * rows * cols, transcendentals=0),
        name="reorder",
    )(order, matrix)


def dot(left, right, left_dim, right_dim):
    return lax.dot_general(
        left, right, (((left_dim,), (right_dim,)), ((), ())), preferred_element_type=f32
    )


def gelu_parts(gate):
    inner = 0.7978845608028654 * (gate + 0.044715 * gate * gate * gate)
    tanh = jnp.tanh(inner)
    slope = 0.5 * (1.0 + tanh) + 0.5 * gate * (1.0 - tanh * tanh) * 0.7978845608028654 * (
        1.0 + 3.0 * 0.044715 * gate * gate
    )
    return 0.5 * gate * (1.0 + tanh), slope


FFN_CHUNK = 256


def ffn_forward(rows, weights, start, out_type):
    tok, width = rows.shape
    units = weights[0].shape[1]
    count, tail = widths(units, FFN_CHUNK)

    def kernel(*refs):
        rows_ref, gate_w, up_w, down_w = refs[:4]
        start_ref = refs[4] if start is not None else None
        gate_ref, up_ref, hidden_ref, out_ref, acc = refs[-5:]
        step = pl.program_id(0)

        @pl.when(step == 0)
        def _():
            acc[...] = jnp.zeros_like(acc) if start_ref is None else start_ref[...]

        def part(size):
            gate = dot(rows_ref[...], gate_w[:, :size], 1, 0)
            up = dot(rows_ref[...], up_w[:, :size], 1, 0)
            inner = 0.7978845608028654 * (gate + 0.044715 * gate * gate * gate)
            hidden = (0.5 * gate * (1.0 + jnp.tanh(inner)) * up).astype(bf16)
            gate_ref[:, :size] = gate.astype(bf16)
            up_ref[:, :size] = up.astype(bf16)
            hidden_ref[:, :size] = hidden
            acc[...] += dot(hidden, down_w[:, :size], 1, 1)

        @pl.when(step < count - 1)
        def _():
            part(FFN_CHUNK)

        @pl.when(step == count - 1)
        def _():
            part(tail)
            out_ref[...] = acc[...].astype(out_type)

    whole = pl.BlockSpec((tok, width), lambda j: (0, 0))
    weight = pl.BlockSpec((width, FFN_CHUNK), lambda j: (0, j))
    side = pl.BlockSpec((tok, FFN_CHUNK), lambda j: (0, j))
    saved = jax.ShapeDtypeStruct((tok, units), bf16)
    operands = (rows,) + tuple(weights) + (() if start is None else (start,))
    gate, up, hidden, out = pl.pallas_call(
        kernel,
        out_shape=(saved, saved, saved, jax.ShapeDtypeStruct((tok, width), out_type)),
        grid_spec=pltpu.PrefetchScalarGridSpec(
            num_scalar_prefetch=0,
            grid=(count,),
            in_specs=[whole, weight, weight, weight] + ([] if start is None else [whole]),
            out_specs=[side, side, side, whole],
            scratch_shapes=[pltpu.VMEM((tok, width), f32)],
        ),
        cost_estimate=pl.CostEstimate(
            flops=6 * tok * width * units,
            bytes_accessed=6 * width * units + 6 * tok * units + 10 * tok * width,
            transcendentals=tok * units,
        ),
        name="ffn_forward",
    )(*operands)
    return (gate, up, hidden), out


def ffn_backward(grad, saved, weights, start, out_type):
    tok, width = grad.shape
    units = weights[0].shape[1]
    count, tail = widths(units, FFN_CHUNK)

    def kernel(*refs):
        grad_ref, gate_ref, up_ref, gate_w, up_w, down_w = refs[:6]
        start_ref = refs[6] if start is not None else None
        d_gate_ref, d_up_ref, out_ref, acc = refs[-4:]
        step = pl.program_id(0)

        @pl.when(step == 0)
        def _():
            acc[...] = jnp.zeros_like(acc) if start_ref is None else start_ref[...]

        def part(size):
            d_hidden = dot(grad_ref[...], down_w[:, :size], 1, 0)
            value, slope = gelu_parts(gate_ref[:, :size].astype(f32))
            d_gate = (d_hidden * up_ref[:, :size].astype(f32) * slope).astype(bf16)
            d_up = (d_hidden * value).astype(bf16)
            d_gate_ref[:, :size] = d_gate
            d_up_ref[:, :size] = d_up
            acc[...] += dot(d_gate, gate_w[:, :size], 1, 1) + dot(d_up, up_w[:, :size], 1, 1)

        @pl.when(step < count - 1)
        def _():
            part(FFN_CHUNK)

        @pl.when(step == count - 1)
        def _():
            part(tail)
            out_ref[...] = acc[...].astype(out_type)

    whole = pl.BlockSpec((tok, width), lambda j: (0, 0))
    weight = pl.BlockSpec((width, FFN_CHUNK), lambda j: (0, j))
    side = pl.BlockSpec((tok, FFN_CHUNK), lambda j: (0, j))
    kept = jax.ShapeDtypeStruct((tok, units), bf16)
    operands = (grad, saved[0], saved[1]) + tuple(weights) + (() if start is None else (start,))
    d_gate, d_up, out = pl.pallas_call(
        kernel,
        out_shape=(kept, kept, jax.ShapeDtypeStruct((tok, width), out_type)),
        grid_spec=pltpu.PrefetchScalarGridSpec(
            num_scalar_prefetch=0,
            grid=(count,),
            in_specs=[whole, side, side, weight, weight, weight]
            + ([] if start is None else [whole]),
            out_specs=[side, side, whole],
            scratch_shapes=[pltpu.VMEM((tok, width), f32)],
        ),
        cost_estimate=pl.CostEstimate(
            flops=6 * tok * width * units,
            bytes_accessed=6 * width * units + 8 * tok * units + 10 * tok * width,
            transcendentals=tok * units,
        ),
        name="ffn_backward",
    )(*operands)
    return (d_gate, d_up), out


GRAD_CHUNK = 512


def weight_grad(lefts, rights, half, other, split):
    rows, tok = lefts[0].shape
    rows //= 2
    units = rights[0].shape[1]
    count, tail = widths(units, GRAD_CHUNK)
    pairs = len(lefts)

    def kernel(*refs):
        left_refs, right_refs = refs[:pairs], refs[pairs : 2 * pairs]
        outs = refs[2 * pairs + (other is not None) :]
        total = dot(left_refs[0][...], right_refs[0][...], 1, 0)
        for left_ref, right_ref in zip(left_refs[1:], right_refs[1:]):
            total = total + dot(left_ref[...], right_ref[...], 1, 0)
        if other is not None:
            total = total + refs[2 * pairs][...].astype(f32)
        total = total.astype(bf16)
        if split is None:
            outs[0][...] = total
        else:
            digits, digit = split
            blocks = 2**digits
            size = rows // blocks
            filled = [0, 0]
            for block in range(blocks):
                side = block >> (digits - 1 - digit) & 1
                outs[side][filled[side] : filled[side] + size] = total[
                    block * size : (block + 1) * size
                ]
                filled[side] += size

    out_rows = rows if split is None else rows // 2
    outs = 1 if split is None else 2
    return pl.pallas_call(
        kernel,
        out_shape=(jax.ShapeDtypeStruct((out_rows, units), bf16),) * outs,
        grid_spec=pltpu.PrefetchScalarGridSpec(
            num_scalar_prefetch=0,
            grid=(count,),
            in_specs=[pl.BlockSpec((rows, tok), lambda j: (half, 0))] * pairs
            + [pl.BlockSpec((tok, GRAD_CHUNK), lambda j: (0, j))] * pairs
            + ([] if other is None else [pl.BlockSpec((rows, GRAD_CHUNK), lambda j: (0, j))]),
            out_specs=[pl.BlockSpec((out_rows, GRAD_CHUNK), lambda j: (0, j))] * outs,
        ),
        cost_estimate=pl.CostEstimate(
            flops=2 * pairs * rows * tok * units,
            bytes_accessed=2 * pairs * tok * (rows + units) + 4 * rows * units,
            transcendentals=0,
        ),
        name="weight_grad",
    )(*lefts, *rights, *(() if other is None else (other,)))


def norm_rows(value, gain_vec):
    return value * lax.rsqrt(jnp.mean(value * value, axis=-1, keepdims=True) + epsilon) * gain_vec


def rotate(value, cos_table, sin_table):
    half_size = value.shape[-1] // 2
    turned = jnp.concatenate([-value[..., half_size:], value[..., :half_size]], axis=-1)
    return value * cos_table + turned * sin_table


def rope_tables(position, head_size):
    inverse_freq = rope_base ** (-jnp.arange(0, head_size, 2, dtype=f32) / head_size)
    angles = position.astype(f32)[:, None] * inverse_freq[None, :]
    angles = jnp.concatenate([angles, angles], axis=-1)
    return (jnp.cos(angles), jnp.sin(angles))


def seq_layout(lengths_row, index):
    seq_ends = jnp.cumsum(lengths_row)
    starts = seq_ends - lengths_row
    segment = jnp.sum((index[:, None] >= seq_ends[None, :]).astype(jnp.int32), axis=1)
    chosen = segment[:, None] == jnp.arange(lengths_row.shape[0], dtype=jnp.int32)[None, :]
    seq_start = jnp.sum(jnp.where(chosen, starts[None, :], 0), axis=1)
    return (segment, index - seq_start)


def visible(seg_query, seg_key, pos_query, pos_key):
    distance = pos_query[:, None] - pos_key[None, :]
    return (seg_query[:, None] == seg_key[None, :]) & (distance >= 0) & (distance < WINDOW)


def masked_scores(queries, key_rows, allowed):
    scale = queries.shape[-1] ** (-0.5)
    scores = jnp.einsum("qhd,kd->hqk", queries, key_rows, preferred_element_type=f32) * scale
    return jnp.where(allowed[None], scores, masked_score)


def attend(queries, key_rows, value_rows, allowed):
    scores = masked_scores(queries, key_rows, allowed)
    row_max = jnp.max(scores, axis=-1, keepdims=True)
    weights_exp = jnp.exp(scores - row_max)
    row_total = jnp.sum(weights_exp, axis=-1, keepdims=True)
    chance = (weights_exp / row_total).astype(bf16)
    mixture = jnp.einsum("hqk,kd->qhd", chance, value_rows, preferred_element_type=f32)
    return (mixture, (row_max + jnp.log(row_total))[..., 0])


def attend_back(queries, key_rows, value_rows, allowed, grad_mix, log_total):
    scale = queries.shape[-1] ** (-0.5)
    scores = masked_scores(queries, key_rows, allowed)
    chance = jnp.exp(scores - log_total[..., None])
    rounded = chance.astype(bf16)
    grad_chance = jnp.einsum("qhd,kd->hqk", grad_mix, value_rows, preferred_element_type=f32)
    inner = jnp.sum(chance * grad_chance, axis=-1, keepdims=True)
    grad_scores = (chance * (grad_chance - inner)).astype(bf16)
    grad_query = jnp.einsum("hqk,kd->qhd", grad_scores, key_rows, preferred_element_type=f32) * scale
    grad_key = jnp.einsum("hqk,qhd->kd", grad_scores, queries, preferred_element_type=f32) * scale
    grad_value = jnp.einsum("hqk,qhd->kd", rounded, grad_mix, preferred_element_type=f32)
    return (grad_query, grad_key, grad_value)


def local(
    tokens, lengths, w_q, w_k, w_v, w_o, w_gate, w_up, w_down,
    g_attn, g_q, g_k, g_post_attn, g_ffn, g_post_ffn, cotangent,
):
    tok, width = tokens.shape
    head_size = w_k.shape[1]
    heads_width = w_q.shape[1]
    heads = heads_width // head_size
    units = w_gate.shape[1]
    groups, shards = lax.axis_size("dp"), lax.axis_size("fsdp")
    group, shard = lax.axis_index("dp"), lax.axis_index("fsdp")
    block = width // groups
    bits = plane_bits()
    order_a, order_b = plane_orders()
    rev = relative_order()
    order = group ^ jnp.asarray(rev)

    w_in = jnp.concatenate([w_q, w_k, w_v], axis=1)
    in_rows, in_cols = w_in.shape[0] // (groups // 2), w_in.shape[1] // 2
    piece = lax.dynamic_slice(w_in, ((group // 2) * in_rows, (group % 2) * in_cols), (in_rows, in_cols))
    table = shards_of(piece, shard)
    table = table.reshape((shards,) + (1,) * len(bits) + table.shape[1:])

    def canonical(part, sequence):
        for bit in sequence:
            other = swap(part, "dp", bit)
            low = (group & bit) == 0
            dim = 1 + len(bits) - 1 - bits.index(bit)
            part = jnp.where(
                low, jnp.concatenate([part, other], dim), jnp.concatenate([other, part], dim)
            )
        return part

    half = shards // 2
    halves = [canonical(table[:half], order_a), canonical(table[half:], order_b)]
    others = [swap(part, "dp", 1) for part in halves]
    low = (group & 1) == 0
    w_in_all = jnp.concatenate(
        [
            jnp.where(
                low, jnp.concatenate([part, other], -1), jnp.concatenate([other, part], -1)
            )
            for part, other in zip(halves, others)
        ]
    ).reshape(width, w_in.shape[1])

    piece = lax.dynamic_slice(w_o, (0, group * block), (w_o.shape[0], block)).T
    piece = shards_of(piece, shard).transpose(1, 0, 2).reshape(block, heads_width)
    w_out = gather_core(
        jnp.concatenate(
            [
                gather_plane(piece[: block // 2], order_a),
                gather_plane(piece[block // 2 :], order_b),
            ],
            axis=-2,
        )
    ).reshape(width, heads_width)

    def own_rows(matrix):
        return lax.dynamic_slice(matrix, (group * block, 0), (block, units))

    down_piece = lax.dynamic_slice(w_down, (0, group * block), (units, block)).T
    pieces = (own_rows(w_gate), own_rows(w_up), down_piece)
    blocks = [
        (
            reorder_rows(w_gate, order, groups),
            reorder_rows(w_up, order, groups),
            reorder_rows(w_down.T, order, groups),
        )
    ]
    for mask in range(2, shards, 2):
        got = [swap(piece, "fsdp", mask) for piece in pieces]
        blocks.append(
            tuple(
                gather_core(gather_plane(part, sequence)).reshape(width, units)
                for part, sequence in zip(got, (order_a, order_b, order_a))
            )
        )

    source = (
        jnp.repeat(order, block, total_repeat_length=width) * block
        + jnp.arange(width, dtype=jnp.int32) % block
    )
    select = (jnp.arange(width, dtype=jnp.int32)[:, None] == source[None, :]).astype(bf16)

    def relative(vec):
        return jnp.take(vec.reshape(groups, block), order, axis=0).reshape(width)

    def natural(vec):
        back = jnp.asarray(np.argsort(rev))
        where = jnp.take(back, group ^ jnp.arange(groups, dtype=jnp.int32))
        return jnp.take(vec.reshape(groups, block), where, axis=0).reshape(width)

    g_pa, g_f, g_pf = relative(g_post_attn), relative(g_ffn), relative(g_post_ffn)
    tokens_rel = jnp.dot(tokens, select, preferred_element_type=f32)
    grad_out = jnp.dot(cotangent, select, preferred_element_type=f32)

    first = shard * tok
    own_index = first + jnp.arange(tok, dtype=jnp.int32)
    prev_index = first - WINDOW + jnp.arange(WINDOW, dtype=jnp.int32)
    seg_own, pos_own = seq_layout(lengths[0], own_index)
    seg_prev, pos_prev = seq_layout(lengths[0], prev_index)
    seg_prev = jnp.where(prev_index < 0, -1, seg_prev)
    allowed = visible(
        seg_own,
        jnp.concatenate([seg_prev, seg_own]),
        pos_own,
        jnp.concatenate([pos_prev, pos_own]),
    )
    cos_table, sin_table = rope_tables(pos_own, head_size)

    def query_map(raw_rows, gain_vec):
        shaped = raw_rows.reshape(tok, heads, head_size)
        return rotate(norm_rows(shaped, gain_vec), cos_table[:, None, :], sin_table[:, None, :])

    def key_map(raw_rows, gain_vec):
        return rotate(norm_rows(raw_rows, gain_vec), cos_table, sin_table)

    inputs = tokens.astype(f32)
    normed_in = norm_rows(inputs, g_attn).astype(bf16)
    raw = jnp.dot(normed_in, w_in_all, preferred_element_type=f32)
    q_raw = raw[:, :heads_width]
    k_raw = raw[:, heads_width : heads_width + head_size]
    v_raw = raw[:, heads_width + head_size :]
    key_rows = key_map(k_raw, g_k).astype(bf16)
    value_rows = v_raw.astype(bf16)
    arrived = passed_along(jnp.stack([key_rows, value_rows]), "fsdp", 1)
    queries = query_map(q_raw, g_q).astype(bf16)
    key_all = jnp.concatenate([arrived[0], key_rows])
    value_all = jnp.concatenate([arrived[1], value_rows])
    mixture, log_total = attend(queries, key_all, value_all, allowed)
    mixture = mixture.reshape(tok, heads_width).astype(bf16)
    attn_out = dot(mixture, w_out, 1, 1)
    residual = tokens_rel + norm_rows(attn_out, g_pa)
    normed_mid = norm_rows(residual, g_f).astype(bf16)

    mid_other = swap(normed_mid, "fsdp", 1)
    saved_own, saved_other = [None] * len(blocks), [None] * len(blocks)
    last = len(blocks) - 1
    acc = None
    saved_own[0], acc = ffn_forward(normed_mid, blocks[0], None, f32)
    acc_other = None
    for i, weights in enumerate(blocks):
        saved_other[i], acc_other = ffn_forward(
            mid_other, weights, acc_other, bf16 if i == last else f32
        )
    branch_got = swap(acc_other, "fsdp", 1)
    for i in range(1, len(blocks)):
        saved_own[i], acc = ffn_forward(normed_mid, blocks[i], acc, f32)
    branch = acc + branch_got.astype(f32)

    output_rel = (residual + norm_rows(branch, g_pf)).astype(bf16)
    output = dot(output_rel, select, 1, 1).astype(bf16)
    pull_post_ffn = jax.vjp(norm_rows, branch, g_pf)[1]
    grad_branch, grad_g_post_ffn = pull_post_ffn(grad_out)
    grad_branch = grad_branch.astype(bf16)
    grad_other = swap(grad_branch, "fsdp", 1)

    grads_own, grads_other = [], []
    acc = acc_other = None
    for i, weights in enumerate(blocks):
        kept, acc = ffn_backward(grad_branch, saved_own[i], weights, acc, f32)
        grads_own.append(kept)
    for i, weights in enumerate(blocks):
        kept, acc_other = ffn_backward(
            grad_other, saved_other[i], weights, acc_other, bf16 if i == last else f32
        )
        grads_other.append(kept)
    mid_got = swap(acc_other, "fsdp", 1)

    mid_t = (normed_mid.T, mid_other.T)
    branch_t = (grad_branch.T, grad_other.T)

    def job(i, kind):
        if kind == 2:
            return branch_t, (saved_own[i][2], saved_other[i][2])
        return mid_t, (grads_own[i][kind], grads_other[i][kind])

    sent = {}
    for i in reversed(range(len(blocks))):
        for kind in (2, 0, 1):
            lefts, rights = job(i, kind)
            (part,) = weight_grad(lefts, rights, 1, None, None)
            sent[i, kind] = swap(part, "dp", 1)
    sums = {}
    for i in reversed(range(len(blocks))):
        for kind in (2, 0, 1):
            lefts, rights = job(i, kind)
            sequence = order_a if (i + kind) % 2 == 0 else order_b
            keep, send = weight_grad(
                lefts, rights, 0, sent[i, kind], (len(bits), bits.index(sequence[0]))
            )
            shape = (2,) * (len(bits) - 1) + (block, units)
            total = reduce_plane(keep.reshape(shape), send.reshape(shape), sequence, bits)
            sums[i, kind] = total
    ffn_grads = []
    for kind in range(3):
        total = sums[0, kind]
        for i in range(1, len(blocks)):
            total = total + swap(sums[i, kind].astype(bf16), "fsdp", 2 * i).astype(f32)
        ffn_grads.append(total if kind < 2 else total.T)

    grad_mid = acc + mid_got.astype(f32)
    pull_ffn_norm = jax.vjp(norm_rows, residual, g_f)[1]
    grad_res_norm, grad_g_ffn = pull_ffn_norm(grad_mid)
    grad_residual = grad_out + grad_res_norm
    pull_post_attn = jax.vjp(norm_rows, attn_out, g_pa)[1]
    grad_attn, grad_g_post_attn = pull_post_attn(grad_residual)
    grad_attn = grad_attn.astype(bf16)
    grad_mixture = jnp.dot(grad_attn, w_out, preferred_element_type=f32).astype(bf16)
    grad_w_out = dot(grad_attn, mixture, 0, 0)
    total = reduce_halves(grad_w_out.reshape(groups, block, heads_width), None)
    grad_w_o = scatter_shards(total, shards, shard).T

    grad_query, grad_key, grad_value = attend_back(
        queries, key_all, value_all, allowed, grad_mixture.reshape(tok, heads, head_size), log_total
    )
    returned = passed_along(
        jnp.stack([grad_key[:WINDOW], grad_value[:WINDOW]]).astype(bf16), "fsdp", -1
    ).astype(f32)
    grad_key_own = grad_key[WINDOW:] + returned[0]
    grad_v_raw = (grad_value[WINDOW:] + returned[1]).astype(bf16)
    grad_q_raw, grad_g_q = jax.vjp(query_map, q_raw, g_q)[1](grad_query)
    grad_k_raw, grad_g_k = jax.vjp(key_map, k_raw, g_k)[1](grad_key_own)
    grad_q_raw = grad_q_raw.astype(bf16)
    grad_k_raw = grad_k_raw.astype(bf16)
    grad_raw = jnp.concatenate([grad_q_raw, grad_k_raw, grad_v_raw], axis=1)

    q_cols, k_cols = heads_width // groups, head_size // groups
    turned = grad_raw.T
    turned = jnp.concatenate(
        [
            turned[:heads_width].reshape(groups, q_cols, tok),
            turned[heads_width : heads_width + head_size].reshape(groups, k_cols, tok),
            turned[heads_width + head_size :].reshape(groups, k_cols, tok),
        ],
        axis=1,
    )
    turned = jnp.take(turned, order, axis=0).reshape(heads_width + 2 * head_size, tok)
    grad_w_in = jnp.dot(turned, normed_in, preferred_element_type=f32)
    total = reduce_halves(grad_w_in.reshape(groups, q_cols + 2 * k_cols, width), None)
    total = scatter_shards(total, shards, shard)
    grad_w_q = total[:q_cols].T
    grad_w_k = total[q_cols : q_cols + k_cols].T
    grad_w_v = total[q_cols + k_cols :].T

    grad_in = dot(grad_raw, w_in_all, 1, 1)
    grad_in_norm, grad_g_attn = jax.vjp(norm_rows, inputs, g_attn)[1](grad_in)
    high = lax.reduce_precision(grad_residual, 8, 7)
    rest = (grad_residual - high).astype(bf16)
    residual_natural = dot(high.astype(bf16), select, 1, 1) + dot(rest, select, 1, 1)
    grad_tokens = (residual_natural + grad_in_norm).astype(bf16)

    gains = jnp.concatenate(
        [
            grad_g_attn,
            grad_g_q,
            grad_g_k,
            natural(grad_g_post_attn),
            natural(grad_g_ffn),
            natural(grad_g_post_ffn),
        ]
    ).reshape(-1, 128)
    for axis in ("dp", "fsdp"):
        bit = 1
        while bit < lax.axis_size(axis):
            gains = gains + swap(gains, axis, bit)
            bit *= 2
    gains = gains.reshape(-1)
    cuts = np.cumsum([width, head_size, head_size, width, width])
    gain_grads = jnp.split(gains, cuts)
    return (
        output, grad_tokens, grad_w_q, grad_w_k, grad_w_v, grad_w_o,
        ffn_grads[0], ffn_grads[1], ffn_grads[2], *gain_grads,
    )


def solution(mesh):
    rows, fsdp = P(("dp", "fsdp"), None), P("fsdp", None)
    in_specs = (
        rows, P("dp", None), fsdp, fsdp, fsdp, fsdp, P(None, "fsdp"), P(None, "fsdp"), fsdp,
        P(), P(), P(), P(), P(), P(), rows,
    )
    cols = P("fsdp", "dp")
    out_specs = (
        rows, rows, cols, cols, cols, cols, P("dp", "fsdp"), P("dp", "fsdp"), cols,
        P(), P(), P(), P(), P(), P(),
    )
    return jax.shard_map(local, mesh=mesh, in_specs=in_specs, out_specs=out_specs, check_vma=False)
```

```python
import functools

import jax
import jax.numpy as jnp
import numpy as np
from jax import lax
from jax.experimental import pallas as pl
from jax.experimental.pallas import tpu as pltpu
from jax.sharding import PartitionSpec as P

WINDOW = 512
epsilon = 1e-06
rope_base = 10000.0
masked_score = -1e30
bf16, f32 = jnp.bfloat16, jnp.float32


def swap(x, axis, mask):
    return lax.ppermute(x, axis, [(i, i ^ mask) for i in range(lax.axis_size(axis))])


def passed_along(x, axis, by):
    length = lax.axis_size(axis)
    pairs = [(i, i + by) for i in range(length) if 0 <= i + by < length]
    return lax.ppermute(x, axis, pairs)


def plane_bits():
    bits, bit = [], 2
    while bit < lax.axis_size("dp"):
        bits.append(bit)
        bit *= 2
    return bits


def relative_order():
    digits = [1] + plane_bits()
    masks = []
    for place in range(lax.axis_size("dp")):
        mask = 0
        for rank, bit in enumerate(digits):
            if place >> (len(digits) - 1 - rank) & 1:
                mask |= bit
        masks.append(mask)
    return np.array(masks, np.int32)


def plane_orders():
    bits = plane_bits()
    return bits, bits[::-1]


def reduce_plane(keep, send, order, bits):
    left = list(bits)
    for place, bit in enumerate(order):
        left.remove(bit)
        got = swap(send, "dp", bit)
        total = keep.astype(f32) + got.astype(f32)
        if place + 1 < len(order):
            following = left.index(order[place + 1])
            keep = lax.index_in_dim(total, 0, following, False).astype(bf16)
            send = lax.index_in_dim(total, 1, following, False).astype(bf16)
    return total


def in_order(pieces, me, axis=0):
    table = jnp.stack(pieces, axis)
    count, bit = len(pieces), 1
    while bit < count:
        shape = table.shape
        view = table.reshape(shape[:axis] + (count // (2 * bit), 2, bit) + shape[axis + 1 :])
        table = jnp.where((me & bit) == 0, view, jnp.flip(view, axis + 1)).reshape(shape)
        bit *= 2
    return table


def reduce_all(keep, send):
    groups, shards = lax.axis_size("dp"), lax.axis_size("fsdp")
    shard = lax.axis_index("fsdp")
    got = swap(send, "dp", 1)
    masks = [int(mask) for mask in relative_order()[: groups // 2]]

    def summed(place):
        return keep[place].astype(f32) + got[place].astype(f32)

    total = summed(0)
    arrived = [swap(summed(i).astype(bf16), "dp", mask) for i, mask in enumerate(masks) if mask]
    for part in arrived:
        total = total + part.astype(f32)
    rows, width = total.shape
    cols = width // shards

    def block(of):
        return lax.dynamic_slice(total, (0, of * cols), (rows, cols))

    out = block(shard)
    arrived = [
        swap(block(shard ^ mask).astype(bf16), "fsdp", mask) for mask in range(1, shards)
    ]
    for part in arrived:
        out = out + part.astype(f32)
    return out


def widths(total, chunk):
    count = -(-total // chunk)
    return count, total - (count - 1) * chunk


def dot(left, right, left_dim, right_dim):
    return lax.dot_general(
        left, right, (((left_dim,), (right_dim,)), ((), ())), preferred_element_type=f32
    )


def gelu_parts(gate):
    square = gate * gate
    tanh = jnp.tanh(gate * (0.7978845608028654 + 0.044715 * 0.7978845608028654 * square))
    half = 0.5 + 0.5 * tanh
    slope = half + half * (1.0 - tanh) * gate * (
        0.7978845608028654 + 3 * 0.044715 * 0.7978845608028654 * square
    )
    return gate * half, slope


def assemble(tables, order, rows):
    half, _, width = tables[0].shape
    lead = tables[0].shape[1] - rows
    groups = 2 * half
    bits = plane_bits()
    rev = relative_order()
    place_a, place_b = np.zeros(half, np.int32), np.zeros(half, np.int32)
    for place in range(half):
        for rank, (first, second) in enumerate(zip(bits, bits[::-1])):
            place_a[place] |= (int(rev[place]) & first > 0) << rank
            place_b[place] |= (int(rev[place]) & second > 0) << rank

    if rows % 8 or lead % 8:
        parts = []
        for side in range(2):
            a = jnp.take(tables[2 * side], place_a, axis=0)
            b = jnp.take(tables[2 * side + 1], place_b, axis=0)
            parts.append(
                (
                    a[:, :rows],
                    b[:, :rows],
                    jnp.concatenate([a[:, rows:], b[:, rows:]], axis=1),
                )
            )
        where = jnp.zeros(groups, jnp.int32).at[order].set(jnp.arange(groups, dtype=jnp.int32))
        return tuple(
            jnp.take(jnp.concatenate(pair), where, axis=0).reshape(groups * rows, width)
            for pair in zip(*parts)
        )

    def kernel(order_ref, a_ref, b_ref, own_a, own_b, other_a, other_b, gate, up, down):
        def fill(left, right):
            gate[...] = left[0, :rows]
            up[...] = right[0, :rows]
            down[:lead] = left[0, rows:]
            down[lead:] = right[0, rows:]

        @pl.when(pl.program_id(0) < half)
        def _():
            fill(own_a, own_b)

        @pl.when(pl.program_id(0) >= half)
        def _():
            fill(other_a, other_b)

    def spec(table, place, first):
        def index(step, order_ref, a_ref, b_ref):
            at = jnp.clip(step - first, 0, half - 1)
            return ((a_ref, b_ref)[place][at], 0, 0)

        return pl.BlockSpec((1,) + table.shape[1:], index)

    result = pl.BlockSpec((rows, width), lambda step, order_ref, a_ref, b_ref: (order_ref[step], 0))
    return pl.pallas_call(
        kernel,
        out_shape=(jax.ShapeDtypeStruct((groups * rows, width), bf16),) * 3,
        grid_spec=pltpu.PrefetchScalarGridSpec(
            num_scalar_prefetch=3,
            grid=(groups,),
            in_specs=[
                spec(table, i % 2, (i // 2) * half) for i, table in enumerate(tables)
            ],
            out_specs=[result] * 3,
        ),
        cost_estimate=pl.CostEstimate(
            flops=0, bytes_accessed=12 * groups * rows * width, transcendentals=0
        ),
        name="assemble",
    )(order, jnp.asarray(place_a), jnp.asarray(place_b), *tables)


FFN_CHUNK = 512


def ffn_forward(rows, weights, start, out_type):
    tok, width = rows.shape
    units = weights[0].shape[0]
    count, tail = widths(units, FFN_CHUNK)

    def kernel(*refs):
        rows_ref, gate_w, up_w, down_w = refs[:4]
        start_ref = refs[4] if start is not None else None
        gate_ref, up_ref, hidden_ref, out_ref, acc = refs[-5:]
        step = pl.program_id(0)

        @pl.when(step == 0)
        def _():
            acc[...] = jnp.zeros_like(acc) if start_ref is None else start_ref[...]

        def part(size):
            gate = dot(rows_ref[...], gate_w[:size], 1, 1)
            up = dot(rows_ref[...], up_w[:size], 1, 1)
            square = gate * gate
            tanh = jnp.tanh(gate * (0.7978845608028654 + 0.044715 * 0.7978845608028654 * square))
            hidden = (gate * (0.5 + 0.5 * tanh) * up).astype(bf16)
            gate_ref[:, :size] = gate.astype(bf16)
            up_ref[:, :size] = up.astype(bf16)
            hidden_ref[:, :size] = hidden
            acc[...] += dot(hidden, down_w[:size], 1, 0)

        @pl.when(step < count - 1)
        def _():
            part(FFN_CHUNK)

        @pl.when(step == count - 1)
        def _():
            part(tail)
            out_ref[...] = acc[...].astype(out_type)

    whole = pl.BlockSpec((tok, width), lambda j: (0, 0))
    weight = pl.BlockSpec((FFN_CHUNK, width), lambda j: (j, 0))
    side = pl.BlockSpec((tok, FFN_CHUNK), lambda j: (0, j))
    saved = jax.ShapeDtypeStruct((tok, units), bf16)
    operands = (rows,) + tuple(weights) + (() if start is None else (start,))
    gate, up, hidden, out = pl.pallas_call(
        kernel,
        out_shape=(saved, saved, saved, jax.ShapeDtypeStruct((tok, width), out_type)),
        grid_spec=pltpu.PrefetchScalarGridSpec(
            num_scalar_prefetch=0,
            grid=(count,),
            in_specs=[whole, weight, weight, weight] + ([] if start is None else [whole]),
            out_specs=[side, side, side, whole],
            scratch_shapes=[pltpu.VMEM((tok, width), f32)],
        ),
        cost_estimate=pl.CostEstimate(
            flops=6 * tok * width * units,
            bytes_accessed=6 * width * units + 6 * tok * units + 10 * tok * width,
            transcendentals=tok * units,
        ),
        name="ffn_forward",
    )(*operands)
    return (gate, up, hidden), out


def ffn_backward(grad, saved, weights, start, out_type):
    tok, width = grad.shape
    units = weights[0].shape[0]
    count, tail = widths(units, FFN_CHUNK)

    def kernel(*refs):
        grad_ref, gate_ref, up_ref, gate_w, up_w, down_w = refs[:6]
        start_ref = refs[6] if start is not None else None
        d_gate_ref, d_up_ref, out_ref, acc = refs[-4:]
        step = pl.program_id(0)

        @pl.when(step == 0)
        def _():
            acc[...] = jnp.zeros_like(acc) if start_ref is None else start_ref[...]

        def part(size):
            d_hidden = dot(grad_ref[...], down_w[:size], 1, 1)
            value, slope = gelu_parts(gate_ref[:, :size].astype(f32))
            d_gate = (d_hidden * up_ref[:, :size].astype(f32) * slope).astype(bf16)
            d_up = (d_hidden * value).astype(bf16)
            d_gate_ref[:, :size] = d_gate
            d_up_ref[:, :size] = d_up
            acc[...] += dot(d_gate, gate_w[:size], 1, 0) + dot(d_up, up_w[:size], 1, 0)

        @pl.when(step < count - 1)
        def _():
            part(FFN_CHUNK)

        @pl.when(step == count - 1)
        def _():
            part(tail)
            out_ref[...] = acc[...].astype(out_type)

    whole = pl.BlockSpec((tok, width), lambda j: (0, 0))
    weight = pl.BlockSpec((FFN_CHUNK, width), lambda j: (j, 0))
    side = pl.BlockSpec((tok, FFN_CHUNK), lambda j: (0, j))
    kept = jax.ShapeDtypeStruct((tok, units), bf16)
    operands = (grad, saved[0], saved[1]) + tuple(weights) + (() if start is None else (start,))
    d_gate, d_up, out = pl.pallas_call(
        kernel,
        out_shape=(kept, kept, jax.ShapeDtypeStruct((tok, width), out_type)),
        grid_spec=pltpu.PrefetchScalarGridSpec(
            num_scalar_prefetch=0,
            grid=(count,),
            in_specs=[whole, side, side, weight, weight, weight]
            + ([] if start is None else [whole]),
            out_specs=[side, side, whole],
            scratch_shapes=[pltpu.VMEM((tok, width), f32)],
        ),
        cost_estimate=pl.CostEstimate(
            flops=6 * tok * width * units,
            bytes_accessed=6 * width * units + 8 * tok * units + 10 * tok * width,
            transcendentals=tok * units,
        ),
        name="ffn_backward",
    )(*operands)
    return (d_gate, d_up), out


def placed_stores(total, segments, size, place_ref, group, keep, send):
    groups = lax.axis_size("dp")

    def fill(mine):
        for block in range(groups):
            out = keep if block % 2 == mine else send
            for first, rows, inside in segments:
                at = pl.multiple_of(place_ref[block] * size + inside, 16)
                out[pl.ds(at, rows)] = total[first + block * rows : first + (block + 1) * rows]

    @pl.when(group % 2 == 0)
    def _():
        fill(0)

    @pl.when(group % 2 == 1)
    def _():
        fill(1)


GRAD_CHUNK = 512


def ffn_weight_grads(mids, branches, triples, places):
    tok, width = mids[0].shape
    units = triples[0][0].shape[1]
    count, _ = widths(units, GRAD_CHUNK)
    groups = lax.axis_size("dp")
    block = width // groups

    def kernel(places_ref, *refs):
        lefts, rights, (keep, send) = refs[:4], refs[4:10], refs[10:]
        kind = pl.program_id(0)
        for which in range(3):

            @pl.when(kind == which)
            def _(which=which):
                left, other = (lefts[0], lefts[1]) if which < 2 else (lefts[2], lefts[3])
                total = dot(left[...], rights[which][...], 0, 0)
                total = total + dot(other[...], rights[3 + which][...], 0, 0)
                placed_stores(
                    total.astype(bf16),
                    ((0, block, 0),),
                    block,
                    places_ref,
                    places_ref[groups],
                    keep.at[0],
                    send.at[0],
                )

    def right(which):
        def index(kind, j, places_ref):
            return (0, jnp.where(kind == which, j, jnp.where(kind < which, 0, count - 1)))

        return pl.BlockSpec((tok, GRAD_CHUNK), index)

    left = pl.BlockSpec((tok, width), lambda kind, j, places_ref: (0, 0))
    half = jax.ShapeDtypeStruct((3, width // 2, units), bf16)
    out = pl.BlockSpec((1, width // 2, GRAD_CHUNK), lambda kind, j, places_ref: (kind, 0, j))
    return pl.pallas_call(
        kernel,
        out_shape=(half, half),
        grid_spec=pltpu.PrefetchScalarGridSpec(
            num_scalar_prefetch=1,
            grid=(3, count),
            in_specs=[left] * 4 + [right(0), right(1), right(2)] * 2,
            out_specs=[out, out],
        ),
        cost_estimate=pl.CostEstimate(
            flops=12 * width * tok * units,
            bytes_accessed=8 * width * tok + 12 * tok * units + 6 * width * units,
            transcendentals=0,
        ),
        name="ffn_weight_grads",
    )(places, *mids, *branches, *triples[0], *triples[1])


def rows_grad(lefts, right, segments, places):
    tok, cols = right.shape
    rows = sum(left.shape[1] for left in lefts)
    groups = lax.axis_size("dp")
    size = rows // groups

    def kernel(places_ref, *refs):
        right_ref, keep, send = refs[-3:]
        for left_ref, own in zip(refs, segments):
            total = dot(left_ref[...], right_ref[...], 0, 0).astype(bf16)
            placed_stores(total, own, size, places_ref, places_ref[groups], keep, send)

    chunk = 512 if cols % 512 == 0 else 384
    half = jax.ShapeDtypeStruct((rows // 2, cols), bf16)
    out = pl.BlockSpec((rows // 2, chunk), lambda j, places_ref: (0, j))
    keep, send = pl.pallas_call(
        kernel,
        out_shape=(half, half),
        grid_spec=pltpu.PrefetchScalarGridSpec(
            num_scalar_prefetch=1,
            grid=(cols // chunk,),
            in_specs=[
                pl.BlockSpec((tok, left.shape[1]), lambda j, places_ref: (0, 0)) for left in lefts
            ]
            + [pl.BlockSpec((tok, chunk), lambda j, places_ref: (0, j))],
            out_specs=[out, out],
        ),
        cost_estimate=pl.CostEstimate(
            flops=2 * rows * tok * cols,
            bytes_accessed=2 * tok * (rows + cols) + 2 * rows * cols,
            transcendentals=0,
        ),
        name="rows_grad",
    )(places, *lefts, right)
    shape = (groups // 2, size, cols)
    return keep.reshape(shape), send.reshape(shape)


def rope_tables(position, head_size):
    inverse_freq = rope_base ** (-jnp.arange(0, head_size, 2, dtype=f32) / head_size)
    angles = position.astype(f32)[:, None] * inverse_freq[None, :]
    return (jnp.cos(angles), jnp.sin(angles))


def seq_layout(lengths_row, index):
    seq_ends = jnp.cumsum(lengths_row)
    starts = seq_ends - lengths_row
    segment = jnp.sum((index[:, None] >= seq_ends[None, :]).astype(jnp.int32), axis=1)
    chosen = segment[:, None] == jnp.arange(lengths_row.shape[0], dtype=jnp.int32)[None, :]
    seq_start = jnp.sum(jnp.where(chosen, starts[None, :], 0), axis=1)
    return (segment, index - seq_start)


def mean_square(value):
    return lax.rsqrt(jnp.mean(value * value, axis=-1, keepdims=True) + epsilon)


def norm_back(value, gain, grad):
    root = mean_square(value)
    scaled = gain * grad
    back = root * scaled - value * (root * root * root) * jnp.mean(
        value * scaled, axis=-1, keepdims=True
    )
    return back, jnp.sum(grad * value * root, axis=0, keepdims=True)


def turn(value, cos, sin):
    half = value.shape[-1] // 2
    low, high = value[:, :half], value[:, half:]
    return jnp.concatenate([low * cos - high * sin, high * cos + low * sin], axis=1)


def turn_back(grad, cos, sin):
    half = grad.shape[-1] // 2
    low, high = grad[:, :half], grad[:, half:]
    return jnp.concatenate([low * cos + high * sin, high * cos - low * sin], axis=1)


def spec(shape, index):
    return pl.BlockSpec(shape, index)


def fixed(array):
    rank = len(array.shape)
    return pl.BlockSpec(array.shape, lambda *step: (0,) * rank)


def call(kernel, name, grid, operands, in_specs, outs, out_specs, scratch, flops, exps=0):
    moved = sum(x.size * x.dtype.itemsize for x in operands)
    moved += sum(x.size * np.dtype(x.dtype).itemsize for x in outs)
    return pl.pallas_call(
        kernel,
        out_shape=tuple(outs),
        grid_spec=pltpu.PrefetchScalarGridSpec(
            num_scalar_prefetch=0,
            grid=grid,
            in_specs=in_specs,
            out_specs=out_specs,
            scratch_shapes=scratch,
        ),
        cost_estimate=pl.CostEstimate(flops=flops, bytes_accessed=moved, transcendentals=exps),
        name=name,
    )(*operands)


def project_in(tokens, w_in, cos, sin, g_attn, g_q, g_k, heads, head):
    tok, width = tokens.shape

    def kernel(x_ref, w_ref, cos_ref, sin_ref, ga, gq, gk, h1, kv, k_raw, q, q_raw):
        step = pl.program_id(0)

        @pl.when(step == 0)
        def _():
            value = x_ref[...].astype(f32)
            h1[...] = (value * mean_square(value) * ga[...]).astype(bf16)

        raw = dot(h1[...], w_ref[...], 1, 0)

        def turned(gain):
            return turn(raw * mean_square(raw) * gain[...], cos_ref[...], sin_ref[...]).astype(bf16)

        @pl.when(step < heads)
        def _():
            q_raw[0] = raw.astype(bf16)
            q[0] = turned(gq)

        @pl.when(step == heads)
        def _():
            k_raw[...] = raw.astype(bf16)
            kv[0] = turned(gk)

        @pl.when(step == heads + 1)
        def _():
            kv[1] = raw.astype(bf16)

    operands = (tokens, w_in, cos, sin, g_attn, g_q, g_k)
    by_head = spec((1, tok, head), lambda j: (jnp.minimum(j, heads - 1), 0, 0))
    outs = (
        jax.ShapeDtypeStruct((tok, width), bf16),
        jax.ShapeDtypeStruct((2, tok, head), bf16),
        jax.ShapeDtypeStruct((tok, head), bf16),
        jax.ShapeDtypeStruct((heads, tok, head), bf16),
        jax.ShapeDtypeStruct((heads, tok, head), bf16),
    )
    return call(
        kernel,
        "project_in",
        (heads + 2,),
        operands,
        [fixed(tokens), spec((width, head), lambda j: (0, j))] + [fixed(x) for x in operands[2:]],
        outs,
        [fixed(x) for x in outs[:3]] + [by_head, by_head],
        [],
        2 * tok * width * w_in.shape[1],
    )


QUERY_ROWS = 128


def window_mask(low_ref, heads):
    rows, cols = WINDOW + QUERY_ROWS, heads * QUERY_ROWS
    key = lax.broadcasted_iota(jnp.int32, (rows, cols), 0)
    query = lax.broadcasted_iota(jnp.int32, (1, cols), 1) % QUERY_ROWS
    low = jnp.concatenate([low_ref[0]] * heads, axis=1)
    return (key >= low) & (key <= query + WINDOW)


def load_window(prev_ref, own_ref, keys, values):
    keys[:WINDOW] = prev_ref[0]
    values[:WINDOW] = prev_ref[1]
    keys[WINDOW:] = own_ref[0]
    values[WINDOW:] = own_ref[1]


def attend(q, kv_prev, kv_own, low, tokens, w_out, g_post, g_ffn):
    heads, tok, head = q.shape
    width = tokens.shape[1]
    blocks = tok // QUERY_ROWS
    cols = heads * QUERY_ROWS

    def kernel(
        q_ref, prev_ref, own_ref, low_ref, x_ref, w_ref, gp, gf,
        mixed, log_sum, attn, residual, h2, keys, values, mixture,
    ):
        step = pl.program_id(0)

        @pl.when(step == 0)
        def _():
            load_window(prev_ref, own_ref, keys, values)

        @pl.when(step < blocks)
        def _():
            first = pl.multiple_of(step * QUERY_ROWS, QUERY_ROWS)
            window = pl.ds(first, WINDOW + QUERY_ROWS)
            scores = dot(keys[window], q_ref[...].reshape(cols, head), 1, 1) * head ** (-0.5)
            scores = jnp.where(window_mask(low_ref, heads), scores, masked_score)
            top = jnp.max(scores, axis=0, keepdims=True)
            chance = jnp.exp(scores - top)
            total = jnp.sum(chance, axis=0, keepdims=True)
            log_sum[0] = top + jnp.log(total)
            chance = (chance * (1.0 / total)).astype(bf16)
            out = dot(chance, values[window], 0, 0).astype(bf16)
            for h in range(heads):
                part = out[h * QUERY_ROWS : (h + 1) * QUERY_ROWS]
                mixed[:, h * head : (h + 1) * head] = part
                mixture[pl.ds(first, QUERY_ROWS), h * head : (h + 1) * head] = part

        @pl.when(step == blocks)
        def _():
            out = dot(mixture[...], w_ref[...], 1, 0)
            attn[...] = out.astype(bf16)
            total = x_ref[...].astype(f32) + out * mean_square(out) * gp[...]
            residual[...] = total
            h2[...] = (total * mean_square(total) * gf[...]).astype(bf16)

    def at(j):
        return jnp.minimum(j, blocks - 1)

    operands = (q, kv_prev, kv_own, low, tokens, w_out, g_post, g_ffn)
    outs = (
        jax.ShapeDtypeStruct((tok, heads * head), bf16),
        jax.ShapeDtypeStruct((blocks, 1, cols), f32),
        jax.ShapeDtypeStruct((tok, width), bf16),
        jax.ShapeDtypeStruct((tok, width), f32),
        jax.ShapeDtypeStruct((tok, width), bf16),
    )
    return call(
        kernel,
        "attend",
        (blocks + 1,),
        operands,
        [
            spec((heads, QUERY_ROWS, head), lambda j: (0, at(j), 0)),
            fixed(kv_prev),
            fixed(kv_own),
            spec((1, 1, QUERY_ROWS), lambda j: (at(j), 0, 0)),
        ]
        + [fixed(x) for x in operands[4:]],
        outs,
        [
            spec((QUERY_ROWS, heads * head), lambda j: (at(j), 0)),
            spec((1, 1, cols), lambda j: (at(j), 0, 0)),
        ]
        + [fixed(x) for x in outs[2:]],
        [
            pltpu.VMEM((2 * WINDOW, head), bf16),
            pltpu.VMEM((2 * WINDOW, head), bf16),
            pltpu.VMEM((tok, heads * head), bf16),
        ],
        4 * heads * tok * 640 * head + 2 * tok * width * heads * head,
        heads * tok * 640,
    )


def after_ffn(own, got, residual, cotangent, g_post):
    tok, width = own.shape
    rows = min(tok, 128)

    def kernel(own_ref, got_ref, res_ref, cot_ref, g_ref, out, d_branch, gain):
        branch = own_ref[...] + got_ref[...].astype(f32)
        out[...] = (res_ref[...] + branch * mean_square(branch) * g_ref[...]).astype(bf16)
        back, part = norm_back(branch, g_ref[...], cot_ref[...].astype(f32))
        d_branch[...] = back.astype(bf16)

        @pl.when(pl.program_id(0) == 0)
        def _():
            gain[...] = jnp.zeros_like(gain)

        gain[...] += part

    block = spec((rows, width), lambda j: (j, 0))
    one = spec((1, width), lambda j: (0, 0))
    outs = (
        jax.ShapeDtypeStruct((tok, width), bf16),
        jax.ShapeDtypeStruct((tok, width), bf16),
        jax.ShapeDtypeStruct((1, width), f32),
    )
    return call(
        kernel,
        "after_ffn",
        (tok // rows,),
        (own, got, residual, cotangent, g_post),
        [block] * 4 + [one],
        outs,
        [block, block, one],
        [],
        30 * tok * width,
    )


def middle_back(own, got, residual, attn, cotangent, g_ffn, g_post, w_out, heads):
    tok, width = own.shape
    head = w_out.shape[0] // heads
    rows = min(tok, 256)

    def kernel(own_ref, got_ref, res_ref, attn_ref, cot_ref, gf, gp, w_ref, d_res, d_attn, d_mixed, gain_f, gain_p):
        @pl.when(pl.program_id(0) == 0)
        def _():
            gain_f[...] = jnp.zeros_like(gain_f)
            gain_p[...] = jnp.zeros_like(gain_p)

        grad = own_ref[...] + got_ref[...].astype(f32)
        back, part = norm_back(res_ref[...], gf[...], grad)
        gain_f[...] += part
        total = cot_ref[...].astype(f32) + back
        d_res[...] = total
        back, part = norm_back(attn_ref[...].astype(f32), gp[...], total)
        gain_p[...] += part
        back = back.astype(bf16)
        d_attn[...] = back
        for h in range(heads):
            d_mixed[h] = dot(back, w_ref[h * head : (h + 1) * head], 1, 1).astype(bf16)

    block = spec((rows, width), lambda j: (j, 0))
    one = spec((1, width), lambda j: (0, 0))
    outs = (
        jax.ShapeDtypeStruct((tok, width), f32),
        jax.ShapeDtypeStruct((tok, width), bf16),
        jax.ShapeDtypeStruct((heads, tok, head), bf16),
        jax.ShapeDtypeStruct((1, width), f32),
        jax.ShapeDtypeStruct((1, width), f32),
    )
    return call(
        kernel,
        "middle_back",
        (tok // rows,),
        (own, got, residual, attn, cotangent, g_ffn, g_post, w_out),
        [block] * 5 + [one, one, fixed(w_out)],
        outs,
        [block, block, spec((heads, rows, head), lambda j: (0, j, 0)), one, one],
        [],
        2 * tok * width * heads * head,
    )


def attend_back(q, kv_prev, kv_own, low, d_mixed, log_sum, q_raw, cos, sin, g_q):
    heads, tok, head = q.shape
    blocks = tok // QUERY_ROWS
    cols = heads * QUERY_ROWS
    scale = head ** (-0.5)

    def kernel(
        q_ref, prev_ref, own_ref, low_ref, dm_ref, log_ref, raw_ref, cos_ref, sin_ref, g_ref,
        d_q, d_prev, d_own, gain, keys, values, d_keys, d_values,
    ):
        step = pl.program_id(0)

        @pl.when(step == 0)
        def _():
            load_window(prev_ref, own_ref, keys, values)
            d_keys[...] = jnp.zeros_like(d_keys)
            d_values[...] = jnp.zeros_like(d_values)
            gain[...] = jnp.zeros_like(gain)

        window = pl.ds(pl.multiple_of(step * QUERY_ROWS, QUERY_ROWS), WINDOW + QUERY_ROWS)
        queries = q_ref[...].reshape(cols, head)
        d_out = dm_ref[...].reshape(cols, head)
        scores = dot(keys[window], queries, 1, 1) * scale
        scores = jnp.where(window_mask(low_ref, heads), scores, masked_score)
        chance = jnp.exp(scores - log_ref[0])
        d_chance = dot(values[window], d_out, 1, 1)
        inner = jnp.sum(chance * d_chance, axis=0, keepdims=True)
        d_scores = (chance * (d_chance - inner)).astype(bf16)
        d_values[window] += dot(chance.astype(bf16), d_out, 1, 0)
        d_keys[window] += dot(d_scores, queries, 1, 0) * scale
        d_query = dot(d_scores, keys[window], 0, 0) * scale
        cos_all = jnp.concatenate([cos_ref[...]] * heads, axis=0)
        sin_all = jnp.concatenate([sin_ref[...]] * heads, axis=0)
        back, part = norm_back(
            raw_ref[...].reshape(cols, head).astype(f32),
            g_ref[...],
            turn_back(d_query, cos_all, sin_all),
        )
        gain[...] += part
        back = back.astype(bf16)
        for h in range(heads):
            d_q[:, h * head : (h + 1) * head] = back[h * QUERY_ROWS : (h + 1) * QUERY_ROWS]

        @pl.when(step == blocks - 1)
        def _():
            d_prev[0] = d_keys[:WINDOW].astype(bf16)
            d_prev[1] = d_values[:WINDOW].astype(bf16)
            d_own[0] = d_keys[WINDOW:]
            d_own[1] = d_values[WINDOW:]

    by_rows = spec((heads, QUERY_ROWS, head), lambda j: (0, j, 0))
    table = spec((QUERY_ROWS, head // 2), lambda j: (j, 0))
    operands = (q, kv_prev, kv_own, low, d_mixed, log_sum, q_raw, cos, sin, g_q)
    outs = (
        jax.ShapeDtypeStruct((tok, heads * head), bf16),
        jax.ShapeDtypeStruct((2, WINDOW, head), bf16),
        jax.ShapeDtypeStruct((2, tok, head), f32),
        jax.ShapeDtypeStruct((1, head), f32),
    )
    return call(
        kernel,
        "attend_back",
        (blocks,),
        operands,
        [
            by_rows,
            fixed(kv_prev),
            fixed(kv_own),
            spec((1, 1, QUERY_ROWS), lambda j: (j, 0, 0)),
            by_rows,
            spec((1, 1, cols), lambda j: (j, 0, 0)),
            by_rows,
            table,
            table,
            fixed(g_q),
        ],
        outs,
        [spec((QUERY_ROWS, heads * head), lambda j: (j, 0))] + [fixed(x) for x in outs[1:]],
        [
            pltpu.VMEM((2 * WINDOW, head), bf16),
            pltpu.VMEM((2 * WINDOW, head), bf16),
            pltpu.VMEM((2 * WINDOW, head), f32),
            pltpu.VMEM((2 * WINDOW, head), f32),
        ],
        10 * heads * tok * 640 * head,
        heads * tok * 640,
    )


def keys_back(d_own, returned, k_raw, cos, sin, g_k):
    _, tok, head = d_own.shape

    def kernel(own_ref, got_ref, raw_ref, cos_ref, sin_ref, g_ref, d_kv, gain):
        grad = own_ref[0] + got_ref[0].astype(f32)
        back, part = norm_back(
            raw_ref[...].astype(f32), g_ref[...], turn_back(grad, cos_ref[...], sin_ref[...])
        )
        gain[...] = part
        d_kv[:, :head] = back.astype(bf16)
        d_kv[:, head:] = (own_ref[1] + got_ref[1].astype(f32)).astype(bf16)

    operands = (d_own, returned, k_raw, cos, sin, g_k)
    outs = (jax.ShapeDtypeStruct((tok, 2 * head), bf16), jax.ShapeDtypeStruct((1, head), f32))
    return call(
        kernel, "keys_back", (1,), operands, [fixed(x) for x in operands], outs,
        [fixed(x) for x in outs], [], 40 * tok * head,
    )


def tokens_back(d_q, d_kv, w_in, tokens, d_res, g_attn):
    tok, width = tokens.shape
    rows = min(tok, 256)
    split = d_q.shape[1]

    def kernel(q_ref, kv_ref, w_ref, x_ref, res_ref, g_ref, out, gain):
        @pl.when(pl.program_id(0) == 0)
        def _():
            gain[...] = jnp.zeros_like(gain)

        grad = dot(q_ref[...], w_ref[:, :split], 1, 1) + dot(kv_ref[...], w_ref[:, split:], 1, 1)
        back, part = norm_back(x_ref[...].astype(f32), g_ref[...], grad)
        gain[...] += part
        out[...] = (res_ref[...] + back).astype(bf16)

    def by_rows(array):
        return spec((rows, array.shape[1]), lambda j: (j, 0))

    outs = (jax.ShapeDtypeStruct((tok, width), bf16), jax.ShapeDtypeStruct((1, width), f32))
    return call(
        kernel,
        "tokens_back",
        (tok // rows,),
        (d_q, d_kv, w_in, tokens, d_res, g_attn),
        [by_rows(d_q), by_rows(d_kv), fixed(w_in), by_rows(tokens), by_rows(d_res), fixed(g_attn)],
        outs,
        [by_rows(tokens), fixed(outs[1])],
        [],
        2 * tok * width * w_in.shape[1],
    )


def local(
    tokens, lengths, w_q, w_k, w_v, w_o, w_gate, w_up, w_down,
    g_attn, g_q, g_k, g_post_attn, g_ffn, g_post_ffn, cotangent,
):
    tok, width = tokens.shape
    head_size = w_k.shape[1]
    heads_width = w_q.shape[1]
    heads = heads_width // head_size
    units = w_gate.shape[1]
    groups, shards = lax.axis_size("dp"), lax.axis_size("fsdp")
    group, shard = lax.axis_index("dp"), lax.axis_index("fsdp")
    block = width // groups
    bits = plane_bits()
    order_a, order_b = plane_orders()
    rev = relative_order()
    order = group ^ jnp.asarray(rev)
    place = jnp.asarray(np.argsort(rev).astype(np.int32) % (groups // 2))
    places = jnp.concatenate(
        [jnp.take(place, group ^ jnp.arange(groups, dtype=jnp.int32)), group[None].astype(jnp.int32)]
    )

    w_in = jnp.concatenate([w_q, w_k, w_v], axis=1)
    in_rows, in_cols = w_in.shape[0] // (groups // 2), w_in.shape[1] // 2
    out_rows, out_side = w_o.shape[0] // groups, width - in_cols
    piece_out = lax.dynamic_slice(w_o, (group * out_rows, 0), (out_rows, width))
    piece = jnp.concatenate(
        [
            lax.dynamic_slice(
                w_in, ((group // 2) * in_rows, (group % 2) * in_cols), (in_rows, in_cols)
            ),
            piece_out[:, :in_cols],
            jnp.concatenate(
                [
                    piece_out[: out_rows // 2, in_cols:],
                    piece_out[out_rows // 2 :, in_cols:],
                ],
                axis=1,
            ),
        ]
    )
    table = in_order(
        [piece] + [swap(piece, "fsdp", mask) for mask in range(1, shards)], shard
    )
    table = in_order(
        [table] + [swap(table, "dp", mask) for mask in range(2, groups, 2)], group // 2, 1
    )
    other = swap(table, "dp", 1)
    mid_rows = in_rows + out_rows

    def both(own, got, axis):
        pair, flipped = jnp.concatenate([own, got], axis), jnp.concatenate([got, own], axis)
        return jnp.where((group & 1) == 0, pair, flipped)

    def out_part(part):
        low_rows = part[:, :, mid_rows:]
        side = jnp.concatenate([low_rows[..., :out_side], low_rows[..., out_side:]], axis=2)
        return jnp.concatenate([part[:, :, in_rows:mid_rows], side], axis=3)[:, :, None]

    w_in_all = both(table[:, :, :in_rows], other[:, :, :in_rows], 3)
    w_in_all = w_in_all.reshape(width, w_in.shape[1])
    w_out = both(out_part(table), out_part(other), 2).reshape(heads_width, width)

    piece_rows = units // groups
    lead = (piece_rows // 2 + 15) // 16 * 16

    def own_rows(matrix, first, rows):
        return lax.dynamic_slice(matrix, (group * piece_rows + first, 0), (rows, width))

    blocks = [(w_gate.T, w_up.T, w_down)]
    piece_a = jnp.concatenate([own_rows(w_gate.T, 0, piece_rows), own_rows(w_down, 0, lead)])
    piece_b = jnp.concatenate(
        [own_rows(w_up.T, 0, piece_rows), own_rows(w_down, lead, piece_rows - lead)]
    )
    for mask in range(2, shards, 2):
        tables = []
        for part, sequence in ((piece_a, order_a), (piece_b, order_b)):
            part = swap(part, "fsdp", mask)[None]
            for bit in sequence:
                part = jnp.concatenate([part, swap(part, "dp", bit)])
            tables.append(part)
        tables += [swap(part, "dp", 1) for part in tables]
        blocks.append(assemble(tables, order, piece_rows))

    first = shard * tok
    own_index = first + jnp.arange(tok, dtype=jnp.int32)
    _, pos_own = seq_layout(lengths[0], own_index)
    at = jnp.arange(tok, dtype=jnp.int32)
    sees = jnp.maximum(WINDOW + at - pos_own, at + 1) - at // QUERY_ROWS * QUERY_ROWS
    sees = sees.reshape(tok // QUERY_ROWS, 1, QUERY_ROWS)
    cos_table, sin_table = rope_tables(pos_own, head_size)
    g_attn, g_q, g_k = g_attn[None], g_q[None], g_k[None]
    g_post_attn, g_ffn, g_post_ffn = g_post_attn[None], g_ffn[None], g_post_ffn[None]

    normed_in, kv_own, k_raw, queries, q_raw = project_in(
        tokens, w_in_all, cos_table, sin_table, g_attn, g_q, g_k, heads, head_size
    )
    kv_prev = passed_along(kv_own, "fsdp", 1)
    mixture, log_sum, attn_out, residual, normed_mid = attend(
        queries, kv_prev, kv_own, sees, tokens, w_out, g_post_attn, g_ffn
    )

    mid_other = swap(normed_mid, "fsdp", 1)
    saved_own, saved_other = [None] * len(blocks), [None] * len(blocks)
    last = len(blocks) - 1
    acc = None
    saved_own[0], acc = ffn_forward(normed_mid, blocks[0], None, f32)
    acc_other = None
    for i, weights in enumerate(blocks):
        saved_other[i], acc_other = ffn_forward(
            mid_other, weights, acc_other, bf16 if i == last else f32
        )
    branch_got = swap(acc_other, "fsdp", 1)
    for i in range(1, len(blocks)):
        saved_own[i], acc = ffn_forward(normed_mid, blocks[i], acc, f32)
    output, grad_branch, grad_g_post_ffn = after_ffn(
        acc, branch_got, residual, cotangent, g_post_ffn
    )
    grad_other = swap(grad_branch, "fsdp", 1)

    grads_own, grads_other = [], []
    acc = acc_other = None
    for i, weights in enumerate(blocks):
        kept, acc = ffn_backward(grad_branch, saved_own[i], weights, acc, f32)
        grads_own.append(kept)
    for i, weights in enumerate(blocks):
        kept, acc_other = ffn_backward(
            grad_other, saved_other[i], weights, acc_other, bf16 if i == last else f32
        )
        grads_other.append(kept)
    mid_got = swap(acc_other, "fsdp", 1)

    sums = []
    for i in reversed(range(len(blocks))):
        keep, send = ffn_weight_grads(
            (normed_mid, mid_other),
            (grad_branch, grad_other),
            (grads_own[i] + saved_own[i][2:], grads_other[i] + saved_other[i][2:]),
            places,
        )
        got = swap(send, "dp", 1)
        shape = (3,) + (2,) * len(bits) + (block, units)
        keep, got = keep.reshape(shape), got.reshape(shape)
        split = ((0, 2), (1,)) if i % 2 == 0 else ((0,), (1, 2))
        total = [None] * 3
        for kinds, sequence in zip(split, (order_a, order_b)):
            low, high = kinds[0], kinds[-1] + 1
            step = max(kinds[-1] - kinds[0], 1)
            first = 1 + bits.index(sequence[0])

            def half_of(side):
                mine = lax.index_in_dim(keep[low:high:step], side, first, False)
                theirs = lax.index_in_dim(got[low:high:step], side, first, False)
                half = (mine.astype(f32) + theirs.astype(f32)).astype(bf16)
                return jnp.moveaxis(half, 0, -3)

            part = reduce_plane(half_of(0), half_of(1), sequence, bits)
            for rank, kind in enumerate(kinds):
                total[kind] = part[rank]
        sums.insert(0, total)
    ffn_grads = sums[0]
    for i in range(1, len(blocks)):
        got = swap(jnp.stack(sums[i]).astype(bf16), "fsdp", 2 * i)
        ffn_grads = [total + part.astype(f32) for total, part in zip(ffn_grads, got)]
    ffn_grads[2] = ffn_grads[2].T

    grad_residual, grad_attn, grad_mixture, grad_g_ffn, grad_g_post_attn = middle_back(
        acc, mid_got, residual, attn_out, cotangent, g_ffn, g_post_attn, w_out, heads
    )
    grad_w_o = reduce_all(*rows_grad((grad_attn,), mixture, (((0, block, 0),),), places)).T
    grad_q, d_prev, d_own, grad_g_q = attend_back(
        queries, kv_prev, kv_own, sees, grad_mixture, log_sum, q_raw, cos_table, sin_table, g_q
    )
    returned = passed_along(d_prev, "fsdp", -1)
    grad_kv, grad_g_k = keys_back(d_own, returned, k_raw, cos_table, sin_table, g_k)
    q_cols, k_cols = heads_width // groups, head_size // groups
    segments = (
        ((0, q_cols, 0),),
        ((0, k_cols, q_cols), (head_size, k_cols, q_cols + k_cols)),
    )
    total = reduce_all(*rows_grad((grad_q, grad_kv), normed_in, segments, places))
    grad_w_q = total[:q_cols].T
    grad_w_k = total[q_cols : q_cols + k_cols].T
    grad_w_v = total[q_cols + k_cols :].T
    grad_tokens, grad_g_attn = tokens_back(
        grad_q, grad_kv, w_in_all, tokens, grad_residual, g_attn
    )

    gains = jnp.concatenate(
        [
            grad_g_attn,
            grad_g_q,
            grad_g_k,
            grad_g_post_attn,
            grad_g_ffn,
            grad_g_post_ffn,
        ],
        axis=1,
    ).reshape(-1, 128)
    for axis in ("dp", "fsdp"):
        bit = 1
        while bit < lax.axis_size(axis):
            gains = gains + swap(gains, axis, bit)
            bit *= 2
    gains = gains.reshape(-1)
    cuts = np.cumsum([width, head_size, head_size, width, width])
    gain_grads = jnp.split(gains, cuts)
    return (
        output, grad_tokens, grad_w_q, grad_w_k, grad_w_v, grad_w_o,
        ffn_grads[0], ffn_grads[1], ffn_grads[2], *gain_grads,
    )


def solution(mesh):
    rows, fsdp = P(("dp", "fsdp"), None), P("fsdp", None)
    in_specs = (
        rows, P("dp", None), fsdp, fsdp, fsdp, fsdp, P(None, "fsdp"), P(None, "fsdp"), fsdp,
        P(), P(), P(), P(), P(), P(), rows,
    )
    cols = P("fsdp", "dp")
    out_specs = (
        rows, rows, cols, cols, cols, cols, P("dp", "fsdp"), P("dp", "fsdp"), cols,
        P(), P(), P(), P(), P(), P(),
    )
    return jax.shard_map(local, mesh=mesh, in_specs=in_specs, out_specs=out_specs, check_vma=False)
```
